32 devices in a mesh: slab: 16 (over z, y, x), sub: 2 (over core).
Axes of the slice: x: 2, y: 2, z: 4, core: 2. Of those that a mesh axis runs over, the one named last changes fastest.
Arguments:
- position: float32 [3, 8192, 128], P(None, ('slab', 'sub')), may hold values from -6 to 6
- state: int32 [8192, 128], P(('slab', 'sub')), may hold values from 0 to 2, as said below
- neighbours: int32 [8192, 8], P(('slab', 'sub')), may hold values from 0 to 8191, as said below
- voxel: int32 [8192, 128], P(('slab', 'sub')), may hold values from 0 to 4194303, as said below
- substrate: float32 [128, 128, 256], P('slab', 'sub'), may hold values from 0.5 to 1.5
- secretion: float32 [128, 128, 256], P('slab', 'sub'), may hold values from 0.2 to 4
Outputs:
- new_position: float32 [3, 8192, 128], P(None, ('slab', 'sub'))
- new_substrate: float32 [128, 128, 256], P('slab', 'sub')
- necrotic_fraction: float32 [], replicated
The draws below stay inside these ranges and needn't reach their ends.
Inputs may be any that keep to these rules, and one draw needn't show every extreme that they name: `state`: 0 marks an empty slot, 1 a live cell, 2 a necrotic cell. `neighbours`: with tiles in blocks of 256 (block t // 256, its slab the block // 2, its part the block % 2): tile t lists itself first, then 8 - 1 different other tiles, each of its own block, of the last 32 tiles of the block 2 blocks before, or of the first 32 tiles of the block 2 blocks after. `voxel`: the cells of a tile of slab s and part u lie in voxels with x from s * 8 to s * 8 + 7 and y from u * 64 to u * 64 + 63.
All inputs are finite; a program needn't handle non-finite values.
Results may differ from the reference program's by a relative error of at most 0.00002.
Values sent between devices are 32-bit elements; how exact they have to be, the bound alone decides.
A program may use at most 64 MiB of HBM per device.

```python
import math
import jax
import jax.numpy as jnp
from jax import lax

TILE = 128
TILES_DEV = 256
NB = 8
GHOST = 32
VX = 8
VY = 64
VZ = 256
SWEEPS = 8
SLABS = 16
SUB_PARTS = 2
TILES = 8192
NX = 128
NY = 128
NZ = 256


def draw_state(key, part):
    tile_index = jnp.arange(TILES)
    block_index = tile_index // TILES_DEV
    slab_index = block_index // SUB_PARTS
    blocks = TILES // TILES_DEV
    base_level = jax.random.randint(jax.random.fold_in(key, 2), (), 100, 300)
    block_jitter = jax.random.randint(jax.random.fold_in(key, 3), (blocks,), 700, 1300)
    ramp = 1000 + 2000 * slab_index // max(SLABS - 1, 1)
    threshold = base_level * ramp // 1000 * jnp.take(block_jitter, block_index) // 1000
    necro_base = jax.random.randint(jax.random.fold_in(key, 4), (), 50, 450)
    necro_jitter = jax.random.randint(jax.random.fold_in(key, 5), (blocks,), 600, 1400)
    necro_level = necro_base * jnp.take(necro_jitter, block_index) // 1000
    draw_level = jax.random.randint(key, (TILES, TILE), 0, 1000)
    necrosis = jax.random.randint(jax.random.fold_in(key, 1), (TILES, TILE), 0, 1000)
    return jnp.where(draw_level < threshold[:, None], jnp.where(necrosis < necro_level[:, None], 2, 1), 0).astype(jnp.int32)


def draw_neighbours(key, part):
    width = TILES_DEV + 2 * GHOST
    tile_index = jnp.arange(TILES)[:, None]
    block_index = tile_index // TILES_DEV
    slab_index = block_index // SUB_PARTS
    position_in = tile_index % TILES_DEV
    slot_index = jnp.arange(width)[None, :]
    below = (block_index - SUB_PARTS) * TILES_DEV + TILES_DEV - GHOST + slot_index
    same_block = block_index * TILES_DEV + slot_index - GHOST
    above = (block_index + SUB_PARTS) * TILES_DEV + slot_index - GHOST - TILES_DEV
    candidate = jnp.where(slot_index < GHOST, below, jnp.where(slot_index < GHOST + TILES_DEV, same_block, above))
    usable = jnp.where(slot_index < GHOST, slab_index > 0, jnp.where(slot_index < GHOST + TILES_DEV, slot_index - GHOST != position_in, slab_index < SLABS - 1))
    scores = jax.random.randint(key, (TILES, width), 0, 2 ** 20) * width + slot_index + jnp.where(usable, 0, 2 ** 30)
    ranking = jnp.argsort(scores, axis=1)[:, :NB - 1]
    chosen = jnp.take_along_axis(candidate, ranking, axis=1)
    return jnp.concatenate([tile_index, chosen], 1).astype(jnp.int32)


def draw_voxel(key, part):
    block_index = jnp.arange(TILES)[:, None] // TILES_DEV
    slab_index = block_index // SUB_PARTS
    part_index = block_index % SUB_PARTS
    offset_x = jax.random.randint(jax.random.fold_in(key, 11), (TILES, TILE), 0, VX)
    offset_y = jax.random.randint(jax.random.fold_in(key, 12), (TILES, TILE), 0, VY)
    offset_z = jax.random.randint(jax.random.fold_in(key, 13), (TILES, TILE), 0, VZ)
    return (((slab_index * VX + offset_x) * NY + part_index * VY + offset_y) * NZ + offset_z).astype(jnp.int32)


def block_scale(own_key, shape, pieces, smallest, high):
    def one(dim, shards_of):
        steps = jax.random.uniform(jax.random.fold_in(jax.random.fold_in(own_key, 6), dim), (shards_of,), jnp.float32, smallest / len(pieces), high / len(pieces))
        return jnp.repeat(jnp.exp(steps), shape[dim] // shards_of).reshape((-1,) + (1,) * (len(shape) - dim - 1))

    gain = one(*pieces[0])
    for cut in pieces[1:]:
        gain = gain * one(*cut)
    return gain


def gaussian(stream_key, extent, deviation, limit, split=(), kind=jnp.bfloat16):
    result = deviation * jax.random.normal(stream_key, extent, jnp.float32)
    if split:
        result = result * block_scale(stream_key, extent, split, -0.22, 0.18)
    return jnp.clip(result, -limit, limit).astype(kind)


def setup_inputs(seed: int = 0) -> dict:
    keys = jax.random.split(jax.random.key(seed), 7)
    return {
        "position": gaussian(keys[0], (3, TILES, TILE), 1.0, 6.0, ((1, 32),), jnp.float32),
        "state": draw_state(jax.random.fold_in(keys[6], 71), 0),
        "neighbours": draw_neighbours(jax.random.fold_in(keys[6], 71), 0),
        "voxel": draw_voxel(jax.random.fold_in(keys[6], 71), 0),
        "substrate": jnp.clip(0.5 + 1.0 * jax.random.uniform(keys[4], (NX, NY, NZ), jnp.float32) ** block_scale(keys[4], (NX, NY, NZ), ((0, 16), (1, 2)), -0.2, 0.2), 0.5, 1.5),
        "secretion": jnp.clip(jnp.exp(math.log(4.0) - 2.9957323 * jax.random.uniform(keys[5], (NX, NY, NZ), jnp.float32) ** block_scale(keys[5], (NX, NY, NZ), ((0, 16), (1, 2)), -0.2, 0.2)), 0.2, 4.0),
    }


SOFTENING = 0.01
REPEL_RADIUS = 2.0
ADHERE_RADIUS = 3.0
REPEL_STRENGTH = 0.05
ADHERE_STRENGTH = 0.02
SPEED_LIMIT = 0.2
SPEED_EPSILON = 1e-06
SUBSTRATE_STEP = 0.5
DECAY_RATE = 0.1
DIFFUSION_NUMBER = 2.0
UPTAKE_SCALE = 0.25

def pair_forces(own_tiles, others):
    delta_x = own_tiles[0][:, :, None] - others[0][:, None, :]
    delta_y = own_tiles[1][:, :, None] - others[1][:, None, :]
    delta_z = own_tiles[2][:, :, None] - others[2][:, None, :]
    distance = jnp.sqrt(delta_x * delta_x + delta_y * delta_y + delta_z * delta_z + SOFTENING)
    repel = REPEL_STRENGTH * jnp.square(jnp.maximum(0.0, 1.0 - distance / REPEL_RADIUS))
    adhere = ADHERE_STRENGTH * jnp.square(jnp.maximum(0.0, 1.0 - distance / ADHERE_RADIUS)) * (own_tiles[4][:, :, None] * others[4][:, None, :])
    weight = own_tiles[3][:, :, None] * others[3][:, None, :] * (repel - adhere) / distance
    return jnp.stack([lax.optimization_barrier(jnp.sum(weight * delta_x, -1)), lax.optimization_barrier(jnp.sum(weight * delta_y, -1)), lax.optimization_barrier(jnp.sum(weight * delta_z, -1))], 0)

def neighbour_sum(padded):
    center = padded[1:-1, 1:-1]
    along_z = jnp.pad(center, ((0, 0), (0, 0), (1, 1)))
    return padded[2:, 1:-1] + padded[:-2, 1:-1] + padded[1:-1, 2:] + padded[1:-1, :-2] + along_z[:, :, 2:] + along_z[:, :, :-2]

def reference(position, state, neighbours, voxel, substrate, secretion):
    occupied = (state > 0).astype(jnp.float32)
    living = (state == 1).astype(jnp.float32)
    features = jnp.concatenate([position, occupied[None], living[None]], 0)
    blocks = TILES // TILES_DEV
    own_blocks = features.reshape(5, blocks, TILES_DEV, TILE).transpose(1, 0, 2, 3)
    id_blocks = neighbours.reshape(blocks, TILES_DEV, NB)

    def one_block(block_item):
        own_tiles, tile_ids = block_item
        others = jnp.take(features, tile_ids.reshape(-1), axis=1).reshape(5, TILES_DEV, NB * TILE)
        return pair_forces(own_tiles, others)
    forces = lax.map(one_block, (own_blocks, id_blocks))
    velocity = forces.transpose(1, 0, 2, 3).reshape(3, TILES, TILE)
    cell_speed = jnp.sqrt(lax.optimization_barrier(jnp.sum(velocity * velocity, 0)))
    fastest = jnp.max(cell_speed)
    step_size = SPEED_LIMIT / (fastest + SPEED_EPSILON)
    new_position = position + step_size * velocity
    live_total = jnp.sum((state == 1).astype(jnp.int32)).astype(jnp.int32)
    necrotic_total = jnp.sum((state == 2).astype(jnp.int32)).astype(jnp.int32)
    live_float = live_total.astype(jnp.float32)
    necrotic_float = necrotic_total.astype(jnp.float32)
    per_cell = UPTAKE_SCALE * (NX * NY * NZ) / live_float
    cell_count = jnp.zeros((NX * NY * NZ,), jnp.float32).at[voxel.reshape(-1)].add(living.reshape(-1)).reshape(NX, NY, NZ)
    diagonal = 1.0 + SUBSTRATE_STEP * DECAY_RATE + 6.0 * DIFFUSION_NUMBER + per_cell * cell_count
    right_side = substrate + SUBSTRATE_STEP * secretion
    concentration = substrate
    for sweep_index in range(SWEEPS):
        padded = jnp.pad(concentration, ((1, 1), (1, 1), (0, 0)))
        concentration = (right_side + DIFFUSION_NUMBER * neighbour_sum(padded)) / diagonal
    necrotic_fraction = necrotic_float / (live_float + necrotic_float)
    return (new_position, concentration, necrotic_fraction)
```

```python
import jax
import jax.numpy as jnp
from jax import lax
from jax.experimental import pallas as pl
from jax.experimental.pallas import tpu as pltpu
from jax.sharding import PartitionSpec as P

TILE = 128
NB = 8
GHOST = 32
SWEEPS = 8


SOFTENING = 0.01
REPEL_RADIUS = 2.0
ADHERE_RADIUS = 3.0
REPEL_STRENGTH = 0.05
ADHERE_STRENGTH = 0.02
SPEED_LIMIT = 0.2
SPEED_EPSILON = 1e-06
SUBSTRATE_STEP = 0.5
DECAY_RATE = 0.1
DIFFUSION_NUMBER = 2.0
UPTAKE_SCALE = 0.25


def with_halo(x, sides, width):
    for axis, dim in sides:
        size, length = (lax.axis_size(axis), x.shape[dim])
        up = [(i, (i + 1) % size) for i in range(size - 1)]
        down = [(j, i) for i, j in up]
        last = lax.slice_in_dim(x, length - width, length, axis=dim)
        initial = lax.slice_in_dim(x, 0, width, axis=dim)
        before = lax.ppermute(last, axis, up)
        after = lax.ppermute(initial, axis, down)
        x = jnp.concatenate([before, x, after], axis=dim)
    return x


FAR = 1.0e6
ROWS = 8
K_ROWS = 64
Q_ROWS = 32
OCCUPIED_ROW = 3
LIMIT_ROW = 4


def split3(x):
    high = x.astype(jnp.bfloat16).astype(jnp.float32)
    rest = x - high
    middle = rest.astype(jnp.bfloat16).astype(jnp.float32)
    return high, middle, rest - middle


def force_rows(base, own):
    row = lax.broadcasted_iota(jnp.int32, base.shape, 0)
    half = jnp.where(row < 3, 0.5 * base, 0.0)
    square = jnp.sum(half * half, axis=0, keepdims=True)
    high, middle, low = split3(half)
    zero = jnp.zeros_like(base)
    if own:
        first, shift = 0, -2.0
    else:
        occupied = base[OCCUPIED_ROW:OCCUPIED_ROW + 1] > 0
        square = jnp.where(occupied, square + 0.25 * SOFTENING, FAR)
        first, shift = 3, 1.0
    norm = jnp.where(row < 6, 1.0, 0.0)
    for r, part in enumerate(split3(square)):
        norm = jnp.where(row == first + r, part, norm)
    if own:
        groups = [high, high, middle, high, low, middle]
    else:
        groups = [high, middle, high, low, high, middle]
    matrix = jnp.concatenate([shift * g for g in groups] + [norm, zero], 0)
    summed = jnp.concatenate([jnp.where(row == 3, 1.0, high), middle, low, zero], 0)
    return matrix.astype(jnp.bfloat16), summed.astype(jnp.bfloat16)


def force_kernel(group, ids, base_ref, out_ref, other_rows, summed_rows, weights, gathered,
                 own_limit):
    width = NB * TILE
    step = pl.program_id(0)

    @pl.when(step == 0)
    def _():
        @pl.loop(0, base_ref.shape[0])
        def _(tile):
            other_rows[tile], summed_rows[tile] = force_rows(base_ref[tile], False)

    for g in range(group):
        me = step * group + g
        own_base = base_ref[GHOST + me]
        own, _ = force_rows(own_base, True)
        own_limit[g] = jnp.broadcast_to(
            own_base[LIMIT_ROW:LIMIT_ROW + 1, :], (TILE, TILE)
        ).T
        for j in range(NB):
            tile = ids[me * NB + j]
            cols = slice(j * TILE, (j + 1) * TILE)
            lows = slice(width + j * TILE, width + (j + 1) * TILE)
            squared = lax.dot_general(
                own, other_rows[tile], (((0,), (0,)), ((), ())),
                preferred_element_type=jnp.float32,
            )
            inverse = lax.rsqrt(squared)
            half_distance = squared * inverse
            repel = jnp.maximum(0.0, 1.0 - half_distance)
            limit = jnp.minimum(own_limit[g], base_ref[tile, LIMIT_ROW:LIMIT_ROW + 1, :])
            adhere = jnp.maximum(0.0, limit - half_distance)
            ratio = ADHERE_STRENGTH / REPEL_STRENGTH * (REPEL_RADIUS / ADHERE_RADIUS) ** 2
            weight = (repel * repel - ratio * (adhere * adhere)) * inverse
            high = weight.astype(jnp.bfloat16)
            low = (weight - high.astype(jnp.float32)).astype(jnp.bfloat16)
            weights[g, :, cols] = high
            weights[g, :, lows] = low
            summed = summed_rows[tile]
            gathered[g, :, cols] = summed
            gathered[g, :, lows] = summed
        sums = lax.dot_general(
            weights[g], gathered[g], (((1,), (1,)), ((), ())),
            preferred_element_type=jnp.float32,
        ).T
        moment = sums[0:ROWS] + sums[ROWS:2 * ROWS] + sums[2 * ROWS:3 * ROWS]
        pull = own_base * moment[3:4] - 2.0 * moment
        occupied = own_base[OCCUPIED_ROW:OCCUPIED_ROW + 1] > 0
        out_ref[g] = jnp.where(occupied, 0.5 * REPEL_STRENGTH * pull, 0.0)


def forces(ghosted, local_ids):
    tiles_dev = local_ids.shape[0]
    all_tiles = ghosted.shape[1]
    group = 4
    state = ghosted[3]
    limits = jnp.where(state == 1, ADHERE_RADIUS / REPEL_RADIUS, -FAR)
    blank = jnp.zeros_like(limits)
    base = jnp.stack(
        [ghosted[0], ghosted[1], ghosted[2], state, limits, blank, blank, blank], 1
    )
    out = pl.pallas_call(
        lambda *refs: force_kernel(group, *refs),
        grid_spec=pltpu.PrefetchScalarGridSpec(
            num_scalar_prefetch=1,
            grid=(tiles_dev // group,),
            in_specs=[pl.BlockSpec((all_tiles, ROWS, TILE), lambda i, ids: (0, 0, 0))],
            out_specs=pl.BlockSpec((group, ROWS, TILE), lambda i, ids: (i, 0, 0)),
            scratch_shapes=[
                pltpu.VMEM((all_tiles, K_ROWS, TILE), jnp.bfloat16),
                pltpu.VMEM((all_tiles, Q_ROWS, TILE), jnp.bfloat16),
                pltpu.VMEM((group, TILE, 2 * NB * TILE), jnp.bfloat16),
                pltpu.VMEM((group, Q_ROWS, 2 * NB * TILE), jnp.bfloat16),
                pltpu.VMEM((group, TILE, TILE), jnp.float32),
            ],
        ),
        out_shape=jax.ShapeDtypeStruct((tiles_dev, ROWS, TILE), jnp.float32),
        cost_estimate=pl.CostEstimate(
            flops=100_000_000_000, bytes_accessed=2_000_000, transcendentals=0
        ),
        name="forces",
    )(local_ids.reshape(-1), base)
    return out[:, :3].transpose(1, 0, 2)


def count_kernel(rows, columns, column_ref, z_ref, out_ref):
    @pl.when(pl.program_id(0) == 0)
    def _():
        out_ref[...] = jnp.zeros_like(out_ref)

    def one_hot(size, ref):
        index = lax.broadcasted_iota(jnp.int32, (size, TILE), 0)
        return jnp.concatenate(
            [
                jnp.where(index == ref[r:r + 1, :], 1.0, 0.0).astype(jnp.bfloat16)
                for r in range(rows)
            ],
            1,
        )

    out_ref[...] += lax.dot_general(
        one_hot(columns, column_ref), one_hot(out_ref.shape[1], z_ref),
        (((1,), (1,)), ((), ())), preferred_element_type=jnp.float32,
    )


def count_cells(column, z, columns, size_z):
    rows = 8
    tiles_dev = column.shape[0]
    spec = pl.BlockSpec((rows, TILE), lambda i: (i, 0))
    return pl.pallas_call(
        lambda *refs: count_kernel(rows, columns, *refs),
        grid=(tiles_dev // rows,),
        in_specs=[spec, spec],
        out_specs=pl.BlockSpec((columns, size_z), lambda i: (0, 0)),
        out_shape=jax.ShapeDtypeStruct((columns, size_z), jnp.float32),
        cost_estimate=pl.CostEstimate(
            flops=20_000_000_000, bytes_accessed=1_000_000, transcendentals=0
        ),
        name="count",
    )(column, z)


def gather_kernel(slab_count, sub_count, mine_ref, all_ref, landed, send_sem, recv_sem):
    me = lax.axis_index("slab") * sub_count + lax.axis_index("sub")
    count = slab_count * sub_count

    def peer(step):
        other = lax.rem(me + step, count)
        return {"slab": other // sub_count, "sub": lax.rem(other, sub_count)}

    barrier = pltpu.get_barrier_semaphore()

    @pl.loop(1, count)
    def _(step):
        pl.semaphore_signal(
            barrier, inc=1, device_id=peer(step), device_id_type=pl.DeviceIdType.MESH
        )

    pl.semaphore_wait(barrier, count - 1)

    def copy(step):
        return pltpu.make_async_remote_copy(
            src_ref=mine_ref,
            dst_ref=landed.at[step],
            send_sem=send_sem.at[step],
            recv_sem=recv_sem.at[step],
            device_id=peer(step),
            device_id_type=pl.DeviceIdType.MESH,
        )

    @pl.loop(1, count)
    def _(step):
        copy(step).start()

    landed[0] = mine_ref[...]

    @pl.loop(1, count)
    def _(step):
        copy(step).wait()

    all_ref[...] = landed[...]


def gather_stats(stats, slab_count, sub_count):
    count = slab_count * sub_count
    vmem = pl.BlockSpec(memory_space=pltpu.VMEM)
    return pl.pallas_call(
        lambda *refs: gather_kernel(slab_count, sub_count, *refs),
        in_specs=[vmem],
        out_specs=vmem,
        out_shape=jax.ShapeDtypeStruct((count,) + stats.shape, stats.dtype),
        scratch_shapes=[
            pltpu.VMEM((count,) + stats.shape, stats.dtype),
            pltpu.SemaphoreType.DMA((count,)),
            pltpu.SemaphoreType.DMA((count,)),
        ],
        compiler_params=pltpu.CompilerParams(collective_id=0, has_side_effects=True),
        cost_estimate=pl.CostEstimate(
            flops=10_000_000_000, bytes_accessed=1_000_000, transcendentals=0
        ),
        name="gather",
    )(stats)


def neighbour_sum(padded):
    center = padded[1:-1, 1:-1]
    along_z = jnp.pad(center, ((0, 0), (0, 0), (1, 1)))
    return (
        padded[2:, 1:-1]
        + padded[:-2, 1:-1]
        + padded[1:-1, 2:]
        + padded[1:-1, :-2]
        + along_z[:, :, 2:]
        + along_z[:, :, :-2]
    )


def body(position, state, neighbours, voxel, substrate, secretion):
    tiles_dev = position.shape[1]
    sub_count = lax.axis_size("sub")
    slab_count = lax.axis_size("slab")
    slab_index = lax.axis_index("slab")
    sub_index = lax.axis_index("sub")
    live_local = jnp.sum((state == 1).astype(jnp.int32))
    necrotic_local = jnp.sum((state == 2).astype(jnp.int32))
    features = jnp.concatenate([position, state.astype(jnp.float32)[None]], 0)
    ghosted = with_halo(features, (("slab", 1),), GHOST)
    first_tile = (slab_index * sub_count + sub_index) * tiles_dev
    below_block = neighbours < first_tile
    above_block = neighbours >= first_tile + tiles_dev
    local_ids = jnp.where(
        below_block,
        neighbours - (first_tile - sub_count * tiles_dev) - (tiles_dev - GHOST),
        jnp.where(
            above_block,
            GHOST + tiles_dev + neighbours - (first_tile + sub_count * tiles_dev),
            GHOST + neighbours - first_tile,
        ),
    )
    velocity = forces(ghosted, local_ids)
    local_fastest = jnp.sqrt(jnp.max(jnp.sum(velocity * velocity, 0)))
    stats = jnp.stack(
        [live_local.astype(jnp.float32), necrotic_local.astype(jnp.float32), local_fastest]
    )
    stats = jnp.broadcast_to(jnp.pad(stats, (0, ROWS - 3))[:, None], (ROWS, TILE))
    everyone = gather_stats(stats, slab_count, sub_count)[:, :, 0]
    live_float = jnp.sum(everyone[:, 0].astype(jnp.int32)).astype(jnp.float32)
    necrotic_float = jnp.sum(everyone[:, 1].astype(jnp.int32)).astype(jnp.float32)
    fastest = jnp.max(everyone[:, 2])
    size_x, size_y, size_z = substrate.shape
    grid_y = size_y * sub_count
    grid_total = size_x * slab_count * grid_y * size_z
    per_cell = UPTAKE_SCALE * grid_total / live_float
    voxel_x = voxel // (grid_y * size_z)
    voxel_y = voxel // size_z % grid_y
    voxel_z = voxel % size_z
    column = (voxel_x - slab_index * size_x) * size_y + (voxel_y - sub_index * size_y)
    column = jnp.where(state == 1, column, -1)
    cell_count = count_cells(column, voxel_z, size_x * size_y, size_z).reshape(substrate.shape)
    right_side = substrate + SUBSTRATE_STEP * secretion
    depth = 4
    sides = (("slab", 1), ("sub", 2))
    wide = with_halo(jnp.stack([substrate, right_side, cell_count]), sides, depth)
    row_index = slab_index * size_x - depth + jnp.arange(size_x + 2 * depth)
    column_index = sub_index * size_y - depth + jnp.arange(size_y + 2 * depth)
    inside_x = (row_index >= 0) & (row_index < size_x * slab_count)
    inside_y = (column_index >= 0) & (column_index < grid_y)
    inside = inside_x[:, None, None] & inside_y[None, :, None]
    diagonal = 1.0 + SUBSTRATE_STEP * DECAY_RATE + 6.0 * DIFFUSION_NUMBER + per_cell * wide[2]
    inverse = jnp.where(inside, 1.0 / diagonal, 0.0)
    right_wide = wide[1] * inverse
    double_inverse = DIFFUSION_NUMBER * inverse
    concentration = wide[0]
    for sweep in range(SWEEPS):
        if sweep and sweep % depth == 0:
            concentration = with_halo(concentration, (("slab", 0), ("sub", 1)), depth)
        cut = sweep % depth + 1
        concentration = (
            right_wide[cut:-cut, cut:-cut]
            + double_inverse[cut:-cut, cut:-cut] * neighbour_sum(concentration)
        )
    step_size = SPEED_LIMIT / (fastest + SPEED_EPSILON)
    new_position = position + step_size * velocity
    necrotic_fraction = necrotic_float / (live_float + necrotic_float)
    return (new_position, concentration, necrotic_fraction)


def solution(mesh):
    return jax.shard_map(
        body,
        mesh=mesh,
        in_specs=(
            P(None, ("slab", "sub"), None),
            P(("slab", "sub"), None),
            P(("slab", "sub"), None),
            P(("slab", "sub"), None),
            P("slab", "sub", None),
            P("slab", "sub", None),
        ),
        out_specs=(P(None, ("slab", "sub"), None), P("slab", "sub", None), P()),
        check_vma=False,
    )
```
